32 devices in a mesh: gx: 8 (over y, x, core), gy: 4 (over z).
Axes of the slice: x: 2, y: 2, z: 4, core: 2. Of those that a mesh axis runs over, the one named last changes fastest.
Arguments:
- control: float32 [4, 128, 128, 128], P(None, 'gy', 'gx'), may hold values from -6 to 6
- level_rate: float32 [4, 128], replicated, may hold values from 0.02 to 0.3
- x_rate: float32 [128], replicated, may hold values from 0.00125 to 0.01875
- y_rate: float32 [128], replicated, may hold values from 0.000625 to 0.009375
- jacobian: float32 [4, 128, 616], replicated, may hold values from -0.25 to 0.25
- innovation: float32 [4096, 616], P(('gx', 'gy')), may hold values from -8 to 8
- predictors: float32 [4096, 8], P(('gx', 'gy')), may hold values from -12 to 12
- bias_coef: float32 [8, 616], replicated, may hold values from -1.8 to 1.8
- inv_var: float32 [616], replicated, may hold values from 0.25 to 4
- obs_tile: int32 [4096, 1], P(('gx', 'gy')), may hold values from 0 to 3; in each aligned block of 128 rows (0 to 127, 128 to 255, ...) at most 32 rows name the same one
- obs_cell: int32 [4096], P(('gx', 'gy')), may hold values from 0 to 511
Outputs:
- obs_gradient: float32 [4, 128, 128, 128], P(None, 'gy', 'gx')
- departures: float32 [4096, 616], P(('gx', 'gy'))
- bias_gradient: float32 [8, 616], replicated
- obs_cost: float32 [], replicated
The draws below stay inside these ranges and needn't reach their ends.
Inputs may be any that keep to these rules, and one draw needn't show every extreme that they name: `obs_tile`: among the 128 observations of one device at most 32 lie in the same latitude tile, and some tile holds exactly 32 of them. `obs_cell`: index of the column within the tile, row by row over 32 rows of 16 columns.
All inputs are finite; a program needn't handle non-finite values.
Results may differ from the reference program's by a relative error of at most 0.000076.
Values sent between devices are 32-bit elements; how exact they have to be, the bound alone decides.
A program may use at most 64 MiB of HBM per device.

```python
import math
import jax
import jax.numpy as jnp
import numpy as np
from jax import lax

V = 4
L = 128
C = 616
P_SIZE = 8
CX = 16
CY = 32
OBS_DEV = 128
CAP = 32
NX = 128
NY = 128
OBS_ALL = 4096
N_GY = 4


def draw_predictors(key, part):
    base_key = jax.random.fold_in(key, 0)
    rows_at = jnp.arange(OBS_ALL, dtype=jnp.float32)[:, None]
    row_scale = 1.0 + 2.0 * rows_at / OBS_ALL
    values = jnp.clip(jax.random.normal(base_key, (OBS_ALL, P_SIZE), jnp.float32), -4.0, 4.0)
    return (values * row_scale).astype(jnp.float32)


def with_ends(values, own_key, least, high):
    place = [jax.random.randint(jax.random.fold_in(own_key, axis), (), 0, length) for axis, length in enumerate(values.shape)]
    longest = values.shape.index(max(values.shape))
    neighbour = place[:longest] + [(place[longest] + 1) % values.shape[longest]] + place[longest + 1:]
    return values.at[tuple(place)].set(least).at[tuple(neighbour)].set(high)


def block_levels(own_key, shape, cuts, least, largest):
    level, own = 1.0, jax.random.fold_in(own_key, 6)
    for axis_at, shards_of in cuts:
        heights = jnp.exp(jax.random.uniform(jax.random.fold_in(own, axis_at), (shards_of,), jnp.float32, least / len(cuts), largest / len(cuts)))
        level = level * jnp.repeat(heights, shape[axis_at] // shards_of).reshape([-1 if axis == axis_at else 1 for axis in range(len(shape))])
    return level


def shared_out(rng, own, number, rows, count, top, reach, skew):
    sequence = jax.random.permutation(rng, count)
    heavy_load, usual = load_shares(count, rows * top, reach, skew, True), load_shares(count, rows * top, reach, skew, False)
    places = jnp.arange(count)

    def named(sizes, turn):
        used = int((sizes > 0).sum())
        fixed = max(1, used // 4)
        passed = fixed + (places - fixed + turn * (used - fixed)) % max(1, count - fixed)
        return jnp.zeros((count,), jnp.int32).at[sequence[jnp.where(places < fixed, places, passed)]].set(jnp.asarray(sizes, jnp.int32))

    sizes = jnp.where(number % 4 == 0, named(heavy_load, number // 4), named(usual, number - number // 4 - 1))
    mixed = jax.random.permutation(jax.random.fold_in(own, 3), count)
    donor, receiver = mixed[0:count // 2 * 2:2], mixed[1:count // 2 * 2:2]
    room = jnp.minimum(sizes[donor] - 1, reach - sizes[receiver]) // 2
    room = jnp.where((donor == sequence[0]) | (receiver == sequence[0]) | (sizes[receiver] == 0), 0, jnp.maximum(room, 0))
    passed = jax.random.randint(jax.random.fold_in(own, 4), (count // 2,), 0, 1 << 20) % (room + 1)
    sizes = sizes.at[donor].add(-passed).at[receiver].add(passed)
    items = jnp.searchsorted(jnp.cumsum(sizes), jnp.arange(rows * top), side="right").astype(jnp.int32)
    listing = items.reshape(top, rows).T
    listing = listing[jax.random.permutation(jax.random.fold_in(own, 1), rows)]
    turn = jax.random.randint(jax.random.fold_in(own, 2), (rows, 1), 0, top)
    return jnp.take_along_axis(listing, (jnp.arange(top)[None, :] + turn) % top, axis=1)


def load_shares(number_of, total, bound, skew, full):
    weights = [(1 << 20) // math.isqrt(grade ** skew) + 1 for grade in range(1, number_of + 1)]
    largest = bound if full else min(bound, max(-(-total // number_of), total * weights[0] // sum(weights)))
    least = 1 if total - largest >= number_of - 1 else 0
    given, surplus = [largest] + [least] * (number_of - 1), total - largest - least * (number_of - 1)
    while surplus > 0:
        free = [i for i in range(1, number_of) if given[i] < largest] or [i for i in range(1, number_of) if given[i] < bound]
        mass, remaining = sum([weights[i] for i in free]), surplus
        for i in free:
            extra = min(bound - given[i], max(1, remaining * weights[i] // mass), surplus)
            given[i] = given[i] + extra
            surplus = surplus - extra
    return np.array(given)


def scatter_about(own_key, dims, spread, most, cuts=(), kind=jnp.bfloat16):
    gain = block_levels(own_key, dims, cuts, -0.22, 0.18) if cuts else 1.0
    entries = jax.random.normal(own_key, dims, jnp.float32) * spread * gain
    return jnp.minimum(jnp.maximum(entries, -most), most).astype(kind)


def setup_inputs(seed: int = 0) -> dict:
    keys = jax.random.split(jax.random.key(seed), 12)
    control = scatter_about(keys[0], (V, NY, NX, L), 1.0, 6.0, ((1, 4), (2, 8)), jnp.float32)
    level_rate = jnp.clip(jnp.exp(jax.random.uniform(keys[1], (V, L), jnp.float32, math.log(0.02), math.log(0.3))), 0.02, 0.3)
    x_rate = jnp.clip(jnp.exp(jax.random.uniform(keys[2], (NX,), jnp.float32, math.log(0.00125), math.log(0.01875))), 0.00125, 0.01875)
    y_rate = jnp.clip(jnp.exp(jax.random.uniform(keys[3], (NY,), jnp.float32, math.log(0.000625), math.log(0.009375))), 0.000625, 0.009375)
    jacobian = scatter_about(keys[4], (V, L, C), (V * L) ** -0.5, 0.25, (), jnp.float32)
    innovation = scatter_about(keys[5], (OBS_ALL, C), 1.0, 8.0, ((0, 32),), jnp.float32)
    predictors = draw_predictors(jax.random.fold_in(keys[11], 71), 0)
    bias_coef = scatter_about(keys[7], (P_SIZE, C), 0.3, 1.8, (), jnp.float32)
    inv_var = jnp.clip(jnp.exp(jax.random.uniform(keys[8], (C,), jnp.float32, math.log(0.25), math.log(4.0))), 0.25, 4.0)
    obs_tile_keys = jax.random.split(jax.random.fold_in(keys[9], 1), OBS_ALL // OBS_DEV)
    obs_tile_turns = jax.random.permutation(jax.random.fold_in(keys[9], 3), OBS_ALL // OBS_DEV)
    obs_tile = jax.vmap(lambda own, number: shared_out(jax.random.fold_in(keys[9], 2), own, number, OBS_DEV, N_GY, 1, CAP, 2))(obs_tile_keys, obs_tile_turns).reshape((OBS_ALL, 1))
    obs_cell = with_ends(jax.random.randint(keys[10], (OBS_ALL,), 0, CY * CX), jax.random.fold_in(keys[10], 1), 0, (CY * CX) - 1).astype(jnp.int32)
    return dict(control=control, level_rate=level_rate, x_rate=x_rate, y_rate=y_rate, jacobian=jacobian, innovation=innovation, predictors=predictors, bias_coef=bias_coef, inv_var=inv_var, obs_tile=obs_tile, obs_cell=obs_cell)


exact_result = lax.Precision.HIGHEST

def causal_pass(moved_state, decays):
    scales = jnp.sqrt(1.0 - decays * decays)

    def advance(running, element):
        current, decay_now, scale_now = element
        running = decay_now * running + scale_now * current
        return (running, running)
    initial = jnp.zeros(moved_state.shape[1:], jnp.float32)
    final_state, result = lax.scan(advance, initial, (moved_state, decays, scales))
    return result

def adjoint_pass(moved_state, decays):
    scales = jnp.sqrt(1.0 - decays * decays)
    following = jnp.concatenate([decays[1:], jnp.zeros_like(decays[:1])], axis=0)

    def advance(running, element):
        current, decay_next = element
        running = current + decay_next * running
        return (running, running)
    initial = jnp.zeros(moved_state.shape[1:], jnp.float32)
    final_state, result = lax.scan(advance, initial, (moved_state, following), reverse=True)
    return scales * result

def along_axis(state, decays, line_axis, pass_fn):
    moved_state = jnp.moveaxis(state, line_axis, 0)
    return jnp.moveaxis(pass_fn(moved_state, decays), 0, line_axis)

def reference(control, level_rate, x_rate, y_rate, jacobian, innovation, predictors, bias_coef, inv_var, obs_tile, obs_cell):
    level_decay = jnp.transpose(1.0 - level_rate)[:, :, None, None]
    x_decay = (1.0 - x_rate)[:, None, None, None]
    y_decay = (1.0 - y_rate)[:, None, None, None]
    state = along_axis(control, level_decay, 3, causal_pass)
    state = along_axis(state, x_decay, 2, causal_pass)
    increment = along_axis(state, y_decay, 1, causal_pass)
    rows_all = jnp.arange(OBS_ALL, dtype=jnp.int32)
    band_of = rows_all // OBS_DEV // N_GY
    lat_row = obs_tile[:, 0] * CY + obs_cell // CX
    lon_col = band_of * CX + obs_cell % CX
    state_profiles = increment[:, lat_row, lon_col, :]
    channel_radiances = jnp.einsum('ziw,zwk->ik', state_profiles, jacobian, precision=exact_result)
    bias_values = jnp.dot(predictors, bias_coef, precision=exact_result)
    departures = innovation - channel_radiances - bias_values
    weighted_departures = departures * inv_var[None, :]
    column_gradients = jnp.einsum('qs,brs->bqr', weighted_departures, jacobian, precision=exact_result)
    grad_field = jnp.zeros_like(increment).at[:, lat_row, lon_col, :].add(column_gradients)
    state = along_axis(grad_field, y_decay, 1, adjoint_pass)
    state = along_axis(state, x_decay, 2, adjoint_pass)
    obs_gradient = along_axis(state, level_decay, 3, adjoint_pass)
    bias_gradient = -jnp.dot(jnp.transpose(predictors), weighted_departures, precision=exact_result) * OBS_ALL ** (-0.5)
    obs_cost = 0.5 * jnp.sum(departures * weighted_departures) / OBS_ALL
    return (obs_gradient, departures, bias_gradient, obs_cost)
```

```python
import functools

import jax
import jax.numpy as jnp
from jax import lax
from jax.experimental import pallas as pl
from jax.experimental.pallas import tpu as pltpu
from jax.sharding import PartitionSpec as P

MESH = pl.DeviceIdType.MESH
F32 = jnp.float32
BF16 = jnp.bfloat16
CUT = -1e30

X_ENDS, X_CORNER, X_CARRY, X_BACK_CORNER, X_BIAS = range(5)
Y_CELLS, Y_ENDS, Y_CORNER, Y_PROF, Y_GRAD, Y_BIAS, Y_CARRY, Y_BACK_CORNER = range(8)


def iota(shape, axis):
    return lax.broadcasted_iota(jnp.int32, shape, axis)


def split(value):
    high = value.astype(BF16)
    return high, (value - high.astype(F32)).astype(BF16)


def mm(left, right, dims):
    return lax.dot_general(left, right, (dims, ((), ())), preferred_element_type=F32)


def mm3(left, right, dims=((1,), (0,))):
    (lh, ll), (rh, rl) = left, right
    return mm(lh, rh, dims) + (mm(lh, rl, dims) + mm(ll, rh, dims))


def to_col(row):
    size = row.shape[1]
    diag = iota((size, size), 0) == iota((size, size), 1)
    return jnp.sum(jnp.where(diag, row, 0.0), axis=1, keepdims=True)


def logs(rates):
    decays = 1.0 - rates
    return jnp.log(decays), 0.5 * jnp.log(1.0 - decays * decays)


def sums_both(row, start):
    size = row.shape[1]
    at0, at1 = iota((size, size), 0), iota((size, size), 1)
    as_row = jnp.sum(jnp.where((at0 <= at1) & (at0 >= start), to_col(row), 0.0), axis=0, keepdims=True)
    as_col = jnp.sum(jnp.where((at1 <= at0) & (at1 >= start), row, 0.0), axis=1, keepdims=True)
    return as_row, as_col


def between(row, me, count, width):
    size = row.shape[1]
    other, lane = iota((count, size), 0), iota((count, size), 1)
    after = (lane >= (other + 1) * width) & (lane < me * width)
    before = (lane >= (me + 1) * width) & (lane < other * width)
    fwd = jnp.exp(jnp.sum(jnp.where(after, row, 0.0), axis=1, keepdims=True))
    bwd = jnp.exp(jnp.sum(jnp.where(before, row, 0.0), axis=1, keepdims=True))
    return fwd, bwd


def kernel(
    nx, ny, control, level_rate, x_rate, y_rate, jacobian, innovation, pred_t, bias_coef, inv_var, tile_row,
    cell_row, grad_out, dep_out, bias_out, cost_out,
    state, jac, innov, state_h, state_l, jf_h, jf_l, decay_x, decay_y, carry,
    x_send, x_recv, y_send, y_recv, c_send, c_recv, c2_send, c2_recv,
    cells_send, cells_recv, prof_send, prof_recv, gsl_send, gsl_recv,
    bx_send, bx_recv, by_send, by_recv, bc_send, bc_recv, bc2_send, bc2_recv,
    b1_recv, b2_recv, b1_send, b2_send, local_sem, sx_sem, rx_sem, sy_sem, ry_sem,
):
    gx, gy = lax.axis_index("gx"), lax.axis_index("gy")
    variables, rows, cols, levels = control.shape
    cells = rows * cols
    channels = innovation.shape[1]
    obs = innovation.shape[0]
    cap = prof_send.shape[1]
    slots = ny * cap
    width = variables * levels
    ends = rows + cols + 8

    loads = [
        pltpu.make_async_copy(control, state, local_sem.at[0]),
        pltpu.make_async_copy(jacobian, jac, local_sem.at[1]),
        pltpu.make_async_copy(innovation, innov, local_sem.at[2]),
    ]
    for load in loads:
        load.start()

    barrier = pltpu.get_barrier_semaphore()

    def each(count, me, act, when):
        def body(t, _):
            @pl.when(when(t, me))
            def _():
                act(t)
            return 0
        lax.fori_loop(0, count, body, 0)

    other = lambda t, me: t != me
    later = lambda t, me: t > me
    earlier = lambda t, me: t < me

    def greet_x(t):
        pl.semaphore_signal(barrier, inc=1, device_id=(t, gy), device_id_type=MESH)

    def greet_y(t):
        pl.semaphore_signal(barrier, inc=1, device_id=(gx, t), device_id_type=MESH)

    each(nx, gx, greet_x, other)
    each(ny, gy, greet_y, other)

    def x_copy(row, src, dst, target, slot):
        return pltpu.make_async_remote_copy(
            src_ref=src, dst_ref=dst.at[slot], send_sem=sx_sem.at[row, target], recv_sem=rx_sem.at[row, slot],
            device_id=(target, gy), device_id_type=MESH)

    def y_copy(row, src, dst, target, slot):
        return pltpu.make_async_remote_copy(
            src_ref=src, dst_ref=dst.at[slot], send_sem=sy_sem.at[row, target], recv_sem=ry_sem.at[row, slot],
            device_id=(gx, target), device_id_type=MESH)

    tile_r = tile_row[...].astype(F32)
    cell_r = cell_row[...].astype(F32)
    tile_c = to_col(tile_r)
    at0, at1 = iota((obs, obs), 0), iota((obs, obs), 1)
    same = tile_c == tile_r
    rank_c = jnp.sum(jnp.where(same & (at1 < at0), 1.0, 0.0), axis=1, keepdims=True)
    rank_r = jnp.sum(jnp.where(same & (at0 < at1), 1.0, 0.0), axis=0, keepdims=True)
    slot_c = (tile_c * cap + rank_c).astype(jnp.int32)
    slot_r = (tile_r * cap + rank_r).astype(jnp.int32)
    placing = jnp.where(slot_c == iota((obs, slots), 1), 1.0, 0.0).astype(BF16)
    placed_t = slot_r == iota((slots, obs), 0)
    placing_t = jnp.where(placed_t, 1.0, 0.0).astype(BF16)
    sent = jnp.sum(jnp.where(placed_t, cell_r + 1.0, 0.0), axis=1, keepdims=True)
    cells_send[...] = jnp.broadcast_to(sent, (slots, 128)).reshape(ny, cap, 128)
    cells_recv[gy] = cells_send[gy]

    x_log, x_scale = logs(x_rate[...])
    y_log, y_scale = logs(y_rate[...])
    fwd, bwd = between(x_log, gx, nx, cols)
    decay_x[0] = jnp.broadcast_to(fwd, (nx, 128))
    decay_x[1] = jnp.broadcast_to(bwd, (nx, 128))
    fwd, bwd = between(y_log, gy, ny, rows)
    decay_y[0] = jnp.broadcast_to(fwd, (ny, 128))
    decay_y[1] = jnp.broadcast_to(bwd, (ny, 128))
    sx_r, sx_c = sums_both(x_log, gx * cols)
    sy_r, sy_c = sums_both(y_log, gy * rows)
    qx_c = sx_c - to_col(x_scale)
    qy_c = sy_c - to_col(y_scale)

    def total(row, start, size):
        lane = iota(row.shape, 1)
        return jnp.sum(jnp.where((lane >= start) & (lane < start + size), row, 0.0), axis=1, keepdims=True)

    t_x, t_y = total(x_log, gx * cols, cols), total(y_log, gy * rows, rows)

    n = iota((1, cells), 1)
    y_n = n // cols
    x_n = n - y_n * cols

    def pick_rows(col, at):
        return jnp.sum(jnp.where(iota((col.shape[0], at.shape[1]), 0) == at, col, 0.0), axis=0, keepdims=True)

    qx_n = pick_rows(qx_c, x_n + gx * cols)
    qy_n = pick_rows(qy_c, y_n + gy * rows)
    e = iota((ends, 1), 0)
    on_x = (e < rows) & (e == y_n)
    on_y = (e >= rows) & (e - rows == x_n) & (e < rows + cols)
    to_x, to_y = t_x - qx_n, t_y - qy_n
    e_log = jnp.where(on_x, to_x, jnp.where(on_y, to_y, jnp.where(e == rows + cols, to_x + to_y, CUT)))
    e_parts = split(jnp.exp(e_log))

    pl.semaphore_wait(barrier, nx + ny - 2)
    each(ny, gy, lambda t: y_copy(Y_CELLS, cells_send.at[t], cells_recv, t, gy).start(), other)

    loads[0].wait()
    for v in range(variables):
        high, low = split(state[v].reshape(cells, levels))
        state_h[:, v * levels:(v + 1) * levels] = high
        state_l[:, v * levels:(v + 1) * levels] = low
    field = (state_h[...], state_l[...])
    tails = mm3(e_parts, field)
    x_send[...] = tails[0:rows]
    y_send[...] = tails[rows:rows + cols]
    c_send[...] = tails[rows + cols:rows + cols + 1]
    each(nx, gx, lambda t: x_copy(X_CORNER, c_send, c_recv, t, gx).start(), later)
    each(nx, gx, lambda t: x_copy(X_ENDS, x_send, x_recv, t, gx).start(), later)
    each(ny, gy, lambda t: y_copy(Y_ENDS, y_send, y_recv, t, gy).start(), later)

    carry[...] = jnp.zeros_like(carry)

    def widen(ref, side, t):
        row = ref[side, pl.ds(t, 1), :]
        return jnp.concatenate([row] * (width // 128), axis=1)

    each(ny, gy, lambda t: y_copy(Y_CELLS, cells_send.at[t], cells_recv, t, t).wait_recv(), other)
    landed = cells_recv[...].reshape(slots, 128)[:, 0:1] - 1.0
    y_s = jnp.floor((landed + 0.5) * (1.0 / cols))
    x_s = (landed - y_s * cols).astype(jnp.int32)
    y_s = jnp.where(landed < 0.0, -5.0, y_s).astype(jnp.int32)

    def pick_cols(row, at):
        return jnp.sum(jnp.where(iota((at.shape[0], row.shape[1]), 1) == at, row, 0.0), axis=1, keepdims=True)

    sx_s = pick_cols(sx_r, x_s + gx * cols)
    sy_s = pick_cols(sy_r, jnp.where(y_s < 0, -1, y_s + gy * rows))
    reach = (y_n <= y_s) & (x_n <= x_s)
    w_cells = split(jnp.exp(jnp.where(reach, (sy_s + sx_s) - (qy_n + qx_n), CUT)))
    c = iota((1, ends), 1)
    qy_e = pick_rows(qy_c, jnp.where(c < rows, c + gy * rows, -1))
    qx_e = pick_rows(qx_c, jnp.where((c >= rows) & (c < rows + cols), c - rows + gx * cols, -1))
    y_e = jnp.where(c < rows, c, -1)
    x_e = jnp.where((c >= rows) & (c < rows + cols), c - rows, -1)
    reach_e = (y_e <= y_s) & (x_e <= x_s) & (y_s >= 0) & (c <= rows + cols)
    w_carry = split(jnp.exp(jnp.where(reach_e, (sy_s + sx_s) - (qy_e + qx_e), CUT)))

    def add_corner(t):
        x_copy(X_CORNER, c_send, c_recv, t, t).wait_recv()
        carry[rows + cols:rows + cols + 1, :] += widen(decay_x, 0, t) * c_recv[t]

    each(nx, gx, add_corner, earlier)
    c2_send[...] = carry[rows + cols:rows + cols + 1, :]
    each(ny, gy, lambda t: y_copy(Y_CORNER, c2_send, c2_recv, t, gy).start(), later)
    carry[rows + cols:rows + cols + 1, :] = jnp.zeros((1, width), F32)

    prof = mm3(w_cells, field)

    loads[1].wait()
    l_log, l_scale = logs(level_rate[...])
    m0, m1 = iota((levels, levels), 0), iota((levels, levels), 1)
    for v in range(variables):
        s_r, s_c = sums_both(l_log[v:v + 1, :], 0)
        q_c = s_c - to_col(l_scale[v:v + 1, :])
        f_t = split(jnp.exp(jnp.where(m0 <= m1, s_r - q_c, CUT)))
        high, low = split(mm3(f_t, split(jac[v])))
        jf_h[v * levels:(v + 1) * levels, :] = high
        jf_l[v * levels:(v + 1) * levels, :] = low

    loads[2].wait()
    pred = split(pred_t[...])
    base = innov[...] - mm3(pred, split(bias_coef[...]), ((0,), (0,)))

    def add_x(t):
        x_copy(X_ENDS, x_send, x_recv, t, t).wait_recv()
        carry[0:rows, :] += widen(decay_x, 0, t) * x_recv[t]

    def add_y(t):
        y_copy(Y_ENDS, y_send, y_recv, t, t).wait_recv()
        carry[rows:rows + cols, :] += widen(decay_y, 0, t) * y_recv[t]

    def add_c2(t):
        y_copy(Y_CORNER, c2_send, c2_recv, t, t).wait_recv()
        carry[rows + cols:rows + cols + 1, :] += widen(decay_y, 0, t) * c2_recv[t]

    each(ny, gy, add_y, earlier)
    each(nx, gx, add_x, earlier)
    each(ny, gy, add_c2, earlier)
    prof = prof + mm3(w_carry, split(carry[...]))
    prof_send[...] = prof.reshape(ny, cap, width)
    each(ny, gy, lambda t: y_copy(Y_PROF, prof_send.at[t], prof_recv, t, gy).start(), other)
    prof_recv[gy] = prof_send[gy]
    each(ny, gy, lambda t: y_copy(Y_PROF, prof_send.at[t], prof_recv, t, t).wait_recv(), other)

    got_h, got_l = split(prof_recv[...].reshape(slots, width))
    nn = ((1,), (0,))
    own = (mm(placing, got_h, nn).astype(BF16), mm(placing, got_l, nn).astype(BF16))
    jf = (jf_h[...], jf_l[...])
    departures = base - mm3(own, jf)
    dep_out[...] = departures
    weighted = departures * inv_var[...]
    w_parts = split(weighted)
    g_h, g_l = split(mm3(w_parts, jf, ((1,), (1,))))
    gsl_send[...] = (mm(placing_t, g_h, nn) + mm(placing_t, g_l, nn)).reshape(ny, cap, width)
    each(ny, gy, lambda t: y_copy(Y_GRAD, gsl_send.at[t], gsl_recv, t, gy).start(), other)
    gsl_recv[gy] = gsl_send[gy]

    b1_send[:, 0:channels] = -mm3(pred, w_parts)
    cost = jnp.sum(jnp.sum(departures * weighted, axis=1, keepdims=True), axis=0, keepdims=True)
    b1_send[:, channels:] = jnp.broadcast_to(0.5 * cost, (b1_send.shape[0], b1_send.shape[1] - channels))
    each(ny, gy, lambda t: y_copy(Y_BIAS, b1_send, b1_recv, t, gy).start(), other)
    b1_recv[gy] = b1_send[...]

    each(ny, gy, lambda t: y_copy(Y_GRAD, gsl_send.at[t], gsl_recv, t, t).wait_recv(), other)
    grads = split(gsl_recv[...].reshape(slots, width))
    tn = ((0,), (0,))
    out = mm3(w_carry, grads, tn)
    bx_send[...] = out[0:rows]
    by_send[...] = out[rows:rows + cols]
    bc_send[...] = out[rows + cols:rows + cols + 1]
    each(nx, gx, lambda t: x_copy(X_BACK_CORNER, bc_send, bc_recv, t, gx).start(), earlier)
    each(nx, gx, lambda t: x_copy(X_CARRY, bx_send, bx_recv, t, gx).start(), earlier)
    each(ny, gy, lambda t: y_copy(Y_CARRY, by_send, by_recv, t, gy).start(), earlier)

    each(ny, gy, lambda t: y_copy(Y_BIAS, b1_send, b1_recv, t, t).wait_recv(), other)
    b2_send[...] = jnp.sum(b1_recv[...], axis=0)
    each(nx, gx, lambda t: x_copy(X_BIAS, b2_send, b2_recv, t, gx).start(), other)
    b2_recv[gx] = b2_send[...]

    carry[...] = jnp.zeros_like(carry)

    def back_corner(t):
        x_copy(X_BACK_CORNER, bc_send, bc_recv, t, t).wait_recv()
        carry[rows + cols:rows + cols + 1, :] += widen(decay_x, 1, t) * bc_recv[t]

    each(nx, gx, back_corner, later)
    bc2_send[...] = carry[rows + cols:rows + cols + 1, :]
    each(ny, gy, lambda t: y_copy(Y_BACK_CORNER, bc2_send, bc2_recv, t, gy).start(), earlier)
    carry[rows + cols:rows + cols + 1, :] = jnp.zeros((1, width), F32)

    here = mm3(w_cells, grads, tn)

    def back_x(t):
        x_copy(X_CARRY, bx_send, bx_recv, t, t).wait_recv()
        carry[0:rows, :] += widen(decay_x, 1, t) * bx_recv[t]

    def back_y(t):
        y_copy(Y_CARRY, by_send, by_recv, t, t).wait_recv()
        carry[rows:rows + cols, :] += widen(decay_y, 1, t) * by_recv[t]

    def back_c2(t):
        y_copy(Y_BACK_CORNER, bc2_send, bc2_recv, t, t).wait_recv()
        carry[rows + cols:rows + cols + 1, :] += widen(decay_y, 1, t) * bc2_recv[t]

    each(ny, gy, back_y, later)
    each(nx, gx, back_x, later)
    each(ny, gy, back_c2, later)
    here = here + mm3(e_parts, split(carry[...]), tn)
    for v in range(variables):
        grad_out[v] = here[:, v * levels:(v + 1) * levels].reshape(rows, cols, levels)

    each(nx, gx, lambda t: x_copy(X_BIAS, b2_send, b2_recv, t, t).wait_recv(), other)
    summed = jnp.sum(b2_recv[...], axis=0)
    obs_total = obs * nx * ny
    bias_out[...] = summed[:, 0:channels] * obs_total ** -0.5
    cost_out[...] = summed[0:1, channels:channels + 1] * (1.0 / obs_total)

    each(ny, gy, lambda t: y_copy(Y_CELLS, cells_send.at[t], cells_recv, t, gy).wait_send(), other)
    each(ny, gy, lambda t: y_copy(Y_PROF, prof_send.at[t], prof_recv, t, gy).wait_send(), other)
    each(ny, gy, lambda t: y_copy(Y_GRAD, gsl_send.at[t], gsl_recv, t, gy).wait_send(), other)
    each(ny, gy, lambda t: y_copy(Y_BIAS, b1_send, b1_recv, t, gy).wait_send(), other)
    each(nx, gx, lambda t: x_copy(X_BIAS, b2_send, b2_recv, t, gx).wait_send(), other)

    def forward_x(t):
        x_copy(X_CORNER, c_send, c_recv, t, gx).wait_send()
        x_copy(X_ENDS, x_send, x_recv, t, gx).wait_send()

    def forward_y(t):
        y_copy(Y_ENDS, y_send, y_recv, t, gy).wait_send()
        y_copy(Y_CORNER, c2_send, c2_recv, t, gy).wait_send()

    def backward_x(t):
        x_copy(X_BACK_CORNER, bc_send, bc_recv, t, gx).wait_send()
        x_copy(X_CARRY, bx_send, bx_recv, t, gx).wait_send()

    def backward_y(t):
        y_copy(Y_CARRY, by_send, by_recv, t, gy).wait_send()
        y_copy(Y_BACK_CORNER, bc2_send, bc2_recv, t, gy).wait_send()

    each(nx, gx, forward_x, later)
    each(ny, gy, forward_y, later)
    each(nx, gx, backward_x, earlier)
    each(ny, gy, backward_y, earlier)


def shards(nx, ny, control, level_rate, x_rate, y_rate, jacobian, innovation, predictors, bias_coef, inv_var,
           obs_tile, obs_cell):
    variables, rows, cols, levels = control.shape
    obs, channels = innovation.shape
    cells, width = rows * cols, variables * levels
    cap = obs // 4
    kinds = predictors.shape[1]
    wide = (channels // 128 + 1) * 128
    ends = rows + cols + 8
    vmem = pl.BlockSpec(memory_space=pltpu.VMEM)
    anyw = pl.BlockSpec(memory_space=pl.ANY)
    both = lambda count, *shape: [pltpu.VMEM(shape, F32), pltpu.VMEM((count,) + shape, F32)]
    slotted = lambda *shape: [pltpu.VMEM((ny, cap) + shape, F32)] * 2
    grad, dep, bias, cost = pl.pallas_call(
        functools.partial(kernel, nx, ny),
        out_shape=(
            jax.ShapeDtypeStruct(control.shape, F32),
            jax.ShapeDtypeStruct(innovation.shape, F32),
            jax.ShapeDtypeStruct((kinds, channels), F32),
            jax.ShapeDtypeStruct((1, 1), F32),
        ),
        in_specs=[anyw, vmem, vmem, vmem, anyw, anyw, vmem, vmem, vmem, vmem, vmem],
        out_specs=(vmem, vmem, vmem, vmem),
        scratch_shapes=[
            pltpu.VMEM(control.shape, F32),
            pltpu.VMEM(jacobian.shape, F32),
            pltpu.VMEM(innovation.shape, F32),
            pltpu.VMEM((cells, width), BF16),
            pltpu.VMEM((cells, width), BF16),
            pltpu.VMEM((width, channels), BF16),
            pltpu.VMEM((width, channels), BF16),
            pltpu.VMEM((2, nx, 128), F32),
            pltpu.VMEM((2, ny, 128), F32),
            pltpu.VMEM((ends, width), F32),
            *both(nx, rows, width), *both(ny, cols, width), *both(nx, 1, width), *both(ny, 1, width),
            *slotted(128), *slotted(width), *slotted(width),
            *both(nx, rows, width), *both(ny, cols, width), *both(nx, 1, width), *both(ny, 1, width),
            pltpu.VMEM((ny, kinds, wide), F32), pltpu.VMEM((nx, kinds, wide), F32),
            pltpu.VMEM((kinds, wide), F32), pltpu.VMEM((kinds, wide), F32),
            pltpu.SemaphoreType.DMA((3,)),
            pltpu.SemaphoreType.DMA((5, nx)), pltpu.SemaphoreType.DMA((5, nx)),
            pltpu.SemaphoreType.DMA((8, ny)), pltpu.SemaphoreType.DMA((8, ny)),
        ],
        compiler_params=pltpu.CompilerParams(
            collective_id=0, has_side_effects=True, vmem_limit_bytes=60 * 1024 * 1024),
    )(control, level_rate, x_rate.reshape(1, -1), y_rate.reshape(1, -1), jacobian, innovation, predictors.T,
      bias_coef, inv_var.reshape(1, -1), obs_tile.reshape(1, -1), obs_cell.reshape(1, -1))
    return grad, dep, bias, cost[0, 0]


def solution(mesh):
    nx, ny = mesh.shape["gx"], mesh.shape["gy"]
    return jax.shard_map(
        functools.partial(shards, nx, ny),
        mesh=mesh,
        in_specs=(
            P(None, "gy", "gx", None),
            P(),
            P(),
            P(),
            P(),
            P(("gx", "gy"), None),
            P(("gx", "gy"), None),
            P(),
            P(),
            P(("gx", "gy"), None),
            P(("gx", "gy")),
        ),
        out_specs=(P(None, "gy", "gx", None), P(("gx", "gy"), None), P(), P()),
        check_vma=False,
    )
```

```python
import functools

import jax
import jax.numpy as jnp
from jax import lax
from jax.experimental import pallas as pl
from jax.experimental.pallas import tpu as pltpu
from jax.sharding import PartitionSpec as P

MESH = pl.DeviceIdType.MESH
F32 = jnp.float32
BF16 = jnp.bfloat16
CUT = -1e30

X_ENDS, X_CORNER, X_CARRY, X_BACK_CORNER, X_BIAS = range(5)
Y_CELLS, Y_ENDS, Y_CORNER, Y_BASE, Y_DEP, Y_BIAS, Y_CARRY, Y_BACK_CORNER = range(8)


def iota(shape, axis):
    return lax.broadcasted_iota(jnp.int32, shape, axis)


def split(value):
    high = value.astype(BF16)
    return high, (value - high.astype(F32)).astype(BF16)


def mm(left, right, dims):
    return lax.dot_general(left, right, (dims, ((), ())), preferred_element_type=F32)


def mm3(left, right, dims=((1,), (0,))):
    (lh, ll), (rh, rl) = left, right
    return mm(lh, rh, dims) + (mm(lh, rl, dims) + mm(ll, rh, dims))


def to_col(row):
    size = row.shape[1]
    diag = iota((size, size), 0) == iota((size, size), 1)
    return jnp.sum(jnp.where(diag, row, 0.0), axis=1, keepdims=True)


def logs(rates):
    decays = 1.0 - rates
    return jnp.log(decays), 0.5 * jnp.log(1.0 - decays * decays)


def sums_both(row, start):
    size = row.shape[1]
    at0, at1 = iota((size, size), 0), iota((size, size), 1)
    as_row = jnp.sum(jnp.where((at0 <= at1) & (at0 >= start), to_col(row), 0.0), axis=0, keepdims=True)
    as_col = jnp.sum(jnp.where((at1 <= at0) & (at1 >= start), row, 0.0), axis=1, keepdims=True)
    return as_row, as_col


def between(row, me, count, width):
    size = row.shape[1]
    other, lane = iota((count, size), 0), iota((count, size), 1)
    after = (lane >= (other + 1) * width) & (lane < me * width)
    before = (lane >= (me + 1) * width) & (lane < other * width)
    fwd = jnp.exp(jnp.sum(jnp.where(after, row, 0.0), axis=1, keepdims=True))
    bwd = jnp.exp(jnp.sum(jnp.where(before, row, 0.0), axis=1, keepdims=True))
    return fwd, bwd


def kernel(
    nx, ny, control, level_rate, x_rate, y_rate, jacobian, innovation, pred_t, bias_coef, inv_var, tile_row,
    cell_row, grad_out, dep_out, bias_out, cost_out,
    state, jac, innov, state_h, state_l, jf_h, jf_l, decay_x, decay_y, carry,
    x_send, x_recv, y_send, y_recv, c_send, c_recv, c2_send, c2_recv,
    cells_send, cells_recv, base_send, base_recv, dsl_send, dsl_recv,
    bx_send, bx_recv, by_send, by_recv, bc_send, bc_recv, bc2_send, bc2_recv,
    b1_recv, b2_recv, b1_send, b2_send, local_sem, sx_sem, rx_sem, sy_sem, ry_sem,
):
    gx, gy = lax.axis_index("gx"), lax.axis_index("gy")
    variables, rows, cols, levels = control.shape
    cells = rows * cols
    channels, obs = innovation.shape
    cap = base_send.shape[1]
    kinds = pred_t.shape[0]
    slots = ny * cap
    width = variables * levels
    ends = rows + cols + 8

    loads = [
        pltpu.make_async_copy(control, state, local_sem.at[0]),
        pltpu.make_async_copy(jacobian, jac, local_sem.at[1]),
        pltpu.make_async_copy(innovation, innov, local_sem.at[2]),
    ]
    for load in loads:
        load.start()

    barrier = pltpu.get_barrier_semaphore()

    def each(count, me, act, when):
        def body(t, _):
            @pl.when(when(t, me))
            def _():
                act(t)
            return 0
        lax.fori_loop(0, count, body, 0)

    other = lambda t, me: t != me
    later = lambda t, me: t > me
    earlier = lambda t, me: t < me

    def greet_x(t):
        pl.semaphore_signal(barrier, inc=1, device_id=(t, gy), device_id_type=MESH)

    def greet_y(t):
        pl.semaphore_signal(barrier, inc=1, device_id=(gx, t), device_id_type=MESH)

    each(nx, gx, greet_x, other)
    each(ny, gy, greet_y, other)

    def x_copy(row, src, dst, target, slot):
        return pltpu.make_async_remote_copy(
            src_ref=src, dst_ref=dst.at[slot], send_sem=sx_sem.at[row, target], recv_sem=rx_sem.at[row, slot],
            device_id=(target, gy), device_id_type=MESH)

    def y_copy(row, src, dst, target, slot):
        return pltpu.make_async_remote_copy(
            src_ref=src, dst_ref=dst.at[slot], send_sem=sy_sem.at[row, target], recv_sem=ry_sem.at[row, slot],
            device_id=(gx, target), device_id_type=MESH)

    tile_r = tile_row[...].astype(F32)
    cell_r = cell_row[...].astype(F32)
    tile_c = to_col(tile_r)
    at0, at1 = iota((obs, obs), 0), iota((obs, obs), 1)
    same = tile_c == tile_r
    rank_r = jnp.sum(jnp.where(same & (at0 < at1), 1.0, 0.0), axis=0, keepdims=True)
    slot_r = (tile_r * cap + rank_r).astype(jnp.int32)
    placed_t = slot_r == iota((slots, obs), 0)
    placing_t = jnp.where(placed_t, 1.0, 0.0).astype(BF16)
    sent = jnp.sum(jnp.where(placed_t, cell_r + 1.0, 0.0), axis=1, keepdims=True)
    cells_send[...] = jnp.broadcast_to(sent, (slots, 128)).reshape(ny, cap, 128)
    cells_recv[gy] = cells_send[gy]

    x_log, x_scale = logs(x_rate[...])
    y_log, y_scale = logs(y_rate[...])
    fwd, bwd = between(x_log, gx, nx, cols)
    decay_x[0] = jnp.broadcast_to(fwd, (nx, 128))
    decay_x[1] = jnp.broadcast_to(bwd, (nx, 128))
    fwd, bwd = between(y_log, gy, ny, rows)
    decay_y[0] = jnp.broadcast_to(fwd, (ny, 128))
    decay_y[1] = jnp.broadcast_to(bwd, (ny, 128))
    sx_r, sx_c = sums_both(x_log, gx * cols)
    sy_r, sy_c = sums_both(y_log, gy * rows)
    qx_c = sx_c - to_col(x_scale)
    qy_c = sy_c - to_col(y_scale)

    def total(row, start, size):
        lane = iota(row.shape, 1)
        return jnp.sum(jnp.where((lane >= start) & (lane < start + size), row, 0.0), axis=1, keepdims=True)

    t_x, t_y = total(x_log, gx * cols, cols), total(y_log, gy * rows, rows)

    n = iota((1, cells), 1)
    y_n = n // cols
    x_n = n - y_n * cols

    def pick_rows(col, at):
        return jnp.sum(jnp.where(iota((col.shape[0], at.shape[1]), 0) == at, col, 0.0), axis=0, keepdims=True)

    qx_n = pick_rows(qx_c, x_n + gx * cols)
    qy_n = pick_rows(qy_c, y_n + gy * rows)
    e = iota((ends, 1), 0)
    on_x = (e < rows) & (e == y_n)
    on_y = (e >= rows) & (e - rows == x_n) & (e < rows + cols)
    to_x, to_y = t_x - qx_n, t_y - qy_n
    e_log = jnp.where(on_x, to_x, jnp.where(on_y, to_y, jnp.where(e == rows + cols, to_x + to_y, CUT)))
    e_parts = split(jnp.exp(e_log))

    pl.semaphore_wait(barrier, nx + ny - 2)
    talk = each
    talk(ny, gy, lambda t: y_copy(Y_CELLS, cells_send.at[t], cells_recv, t, gy).start(), other)

    loads[0].wait()
    for v in range(variables):
        high, low = split(state[v].reshape(cells, levels))
        state_h[:, v * levels:(v + 1) * levels] = high
        state_l[:, v * levels:(v + 1) * levels] = low
    field = (state_h[...], state_l[...])
    tails = mm3(e_parts, field)
    x_send[...] = tails[0:rows]
    y_send[...] = tails[rows:rows + cols]
    c_send[...] = tails[rows + cols:rows + cols + 1]
    talk(nx, gx, lambda t: x_copy(X_CORNER, c_send, c_recv, t, gx).start(), later)
    talk(nx, gx, lambda t: x_copy(X_ENDS, x_send, x_recv, t, gx).start(), later)
    talk(ny, gy, lambda t: y_copy(Y_ENDS, y_send, y_recv, t, gy).start(), later)

    nn, nt, tn = ((1,), (0,)), ((1,), (1,)), ((0,), (0,))
    loads[2].wait()
    pred = split(pred_t[...])
    base_parts = split(innov[...] - mm3(split(bias_coef[...]), pred, tn))
    to_slots = lambda parts: mm(placing_t, parts[0], nt) + mm(placing_t, parts[1], nt)
    base_send[:, :, 0:channels] = to_slots(base_parts).reshape(ny, cap, channels)
    base_send[:, :, channels:channels + kinds] = to_slots(pred).reshape(ny, cap, kinds)
    rest = base_send.shape[2] - channels - kinds
    base_send[:, :, channels + kinds:] = jnp.zeros((ny, cap, rest), F32)
    talk(ny, gy, lambda t: y_copy(Y_BASE, base_send.at[t], base_recv, t, gy).start(), other)
    base_recv[gy] = base_send[gy]

    carry[...] = jnp.zeros_like(carry)

    def widen(ref, side, t):
        row = ref[side, pl.ds(t, 1), :]
        return jnp.concatenate([row] * (width // 128), axis=1)

    talk(ny, gy, lambda t: y_copy(Y_CELLS, cells_send.at[t], cells_recv, t, t).wait_recv(), other)
    landed = cells_recv[...].reshape(slots, 128)[:, 0:1] - 1.0
    y_s = jnp.floor((landed + 0.5) * (1.0 / cols))
    x_s = (landed - y_s * cols).astype(jnp.int32)
    y_s = jnp.where(landed < 0.0, -5.0, y_s).astype(jnp.int32)

    def pick_cols(row, at):
        return jnp.sum(jnp.where(iota((at.shape[0], row.shape[1]), 1) == at, row, 0.0), axis=1, keepdims=True)

    sx_s = pick_cols(sx_r, x_s + gx * cols)
    sy_s = pick_cols(sy_r, jnp.where(y_s < 0, -1, y_s + gy * rows))
    reach = (y_n <= y_s) & (x_n <= x_s)
    w_cells = split(jnp.exp(jnp.where(reach, (sy_s + sx_s) - (qy_n + qx_n), CUT)))
    c = iota((1, ends), 1)
    qy_e = pick_rows(qy_c, jnp.where(c < rows, c + gy * rows, -1))
    qx_e = pick_rows(qx_c, jnp.where((c >= rows) & (c < rows + cols), c - rows + gx * cols, -1))
    y_e = jnp.where(c < rows, c, -1)
    x_e = jnp.where((c >= rows) & (c < rows + cols), c - rows, -1)
    reach_e = (y_e <= y_s) & (x_e <= x_s) & (y_s >= 0) & (c <= rows + cols)
    w_carry = split(jnp.exp(jnp.where(reach_e, (sy_s + sx_s) - (qy_e + qx_e), CUT)))

    def add_corner(t):
        x_copy(X_CORNER, c_send, c_recv, t, t).wait_recv()
        carry[rows + cols:rows + cols + 1, :] += widen(decay_x, 0, t) * c_recv[t]

    talk(nx, gx, add_corner, earlier)
    c2_send[...] = carry[rows + cols:rows + cols + 1, :]
    talk(ny, gy, lambda t: y_copy(Y_CORNER, c2_send, c2_recv, t, gy).start(), later)
    carry[rows + cols:rows + cols + 1, :] = jnp.zeros((1, width), F32)

    prof = mm3(w_cells, field)

    loads[1].wait()
    l_log, l_scale = logs(level_rate[...])
    m0, m1 = iota((levels, levels), 0), iota((levels, levels), 1)
    for v in range(variables):
        s_r, s_c = sums_both(l_log[v:v + 1, :], 0)
        q_r = s_r - l_scale[v:v + 1, :]
        f_v = split(jnp.exp(jnp.where(m1 <= m0, s_c - q_r, CUT)))
        high, low = split(mm3(split(jac[v]), f_v))
        jf_h[:, v * levels:(v + 1) * levels] = high
        jf_l[:, v * levels:(v + 1) * levels] = low

    def add_x(t):
        x_copy(X_ENDS, x_send, x_recv, t, t).wait_recv()
        carry[0:rows, :] += widen(decay_x, 0, t) * x_recv[t]

    def add_y(t):
        y_copy(Y_ENDS, y_send, y_recv, t, t).wait_recv()
        carry[rows:rows + cols, :] += widen(decay_y, 0, t) * y_recv[t]

    def add_c2(t):
        y_copy(Y_CORNER, c2_send, c2_recv, t, t).wait_recv()
        carry[rows + cols:rows + cols + 1, :] += widen(decay_y, 0, t) * c2_recv[t]

    talk(ny, gy, add_y, earlier)
    talk(nx, gx, add_x, earlier)
    talk(ny, gy, add_c2, earlier)
    prof = prof + mm3(w_carry, split(carry[...]))
    talk(ny, gy, lambda t: y_copy(Y_BASE, base_send.at[t], base_recv, t, t).wait_recv(), other)
    arrived = base_recv[...]
    jf = (jf_h[...], jf_l[...])
    departures = arrived[:, :, 0:channels].reshape(slots, channels) - mm3(split(prof), jf, nt)
    dsl_send[...] = departures.reshape(ny, cap, channels)
    weighted = departures * inv_var[...].reshape(1, channels)
    w_parts = split(weighted)
    grads = split(mm3(w_parts, jf))
    out = mm3(w_carry, grads, tn)
    bx_send[...] = out[0:rows]
    by_send[...] = out[rows:rows + cols]
    bc_send[...] = out[rows + cols:rows + cols + 1]
    talk(nx, gx, lambda t: x_copy(X_BACK_CORNER, bc_send, bc_recv, t, gx).start(), earlier)
    talk(nx, gx, lambda t: x_copy(X_CARRY, bx_send, bx_recv, t, gx).start(), earlier)
    talk(ny, gy, lambda t: y_copy(Y_CARRY, by_send, by_recv, t, gy).start(), earlier)

    b1_send[:, 0:channels] = -mm3(split(arrived[:, :, channels:channels + kinds].reshape(slots, kinds)), w_parts, tn)
    cost = jnp.sum(jnp.sum(departures * weighted, axis=1, keepdims=True), axis=0, keepdims=True)
    b1_send[:, channels:] = jnp.broadcast_to(0.5 * cost, (b1_send.shape[0], b1_send.shape[1] - channels))
    talk(ny, gy, lambda t: y_copy(Y_BIAS, b1_send, b1_recv, t, gy).start(), other)
    b1_recv[gy] = b1_send[...]

    talk(ny, gy, lambda t: y_copy(Y_DEP, dsl_send.at[t], dsl_recv, t, gy).start(), other)
    dsl_recv[gy] = dsl_send[gy]

    talk(ny, gy, lambda t: y_copy(Y_BIAS, b1_send, b1_recv, t, t).wait_recv(), other)
    b2_send[...] = jnp.sum(b1_recv[...], axis=0)
    talk(nx, gx, lambda t: x_copy(X_BIAS, b2_send, b2_recv, t, gx).start(), other)
    b2_recv[gx] = b2_send[...]

    carry[...] = jnp.zeros_like(carry)

    def back_corner(t):
        x_copy(X_BACK_CORNER, bc_send, bc_recv, t, t).wait_recv()
        carry[rows + cols:rows + cols + 1, :] += widen(decay_x, 1, t) * bc_recv[t]

    talk(nx, gx, back_corner, later)
    bc2_send[...] = carry[rows + cols:rows + cols + 1, :]
    talk(ny, gy, lambda t: y_copy(Y_BACK_CORNER, bc2_send, bc2_recv, t, gy).start(), earlier)
    carry[rows + cols:rows + cols + 1, :] = jnp.zeros((1, width), F32)

    here = mm3(w_cells, grads, tn)

    talk(ny, gy, lambda t: y_copy(Y_DEP, dsl_send.at[t], dsl_recv, t, t).wait_recv(), other)
    d_h, d_l = split(dsl_recv[...].reshape(slots, channels))
    dep_out[...] = mm(d_h, placing_t, tn) + mm(d_l, placing_t, tn)

    def back_x(t):
        x_copy(X_CARRY, bx_send, bx_recv, t, t).wait_recv()
        carry[0:rows, :] += widen(decay_x, 1, t) * bx_recv[t]

    def back_y(t):
        y_copy(Y_CARRY, by_send, by_recv, t, t).wait_recv()
        carry[rows:rows + cols, :] += widen(decay_y, 1, t) * by_recv[t]

    def back_c2(t):
        y_copy(Y_BACK_CORNER, bc2_send, bc2_recv, t, t).wait_recv()
        carry[rows + cols:rows + cols + 1, :] += widen(decay_y, 1, t) * bc2_recv[t]

    talk(ny, gy, back_y, later)
    talk(nx, gx, back_x, later)
    talk(ny, gy, back_c2, later)
    here = here + mm3(e_parts, split(carry[...]), tn)
    for v in range(variables):
        grad_out[v] = here[:, v * levels:(v + 1) * levels].reshape(rows, cols, levels)

    talk(nx, gx, lambda t: x_copy(X_BIAS, b2_send, b2_recv, t, t).wait_recv(), other)
    summed = jnp.sum(b2_recv[...], axis=0)
    obs_total = obs * nx * ny
    bias_out[...] = summed[:, 0:channels] * obs_total ** -0.5
    cost_out[...] = summed[0:1, channels:channels + 1] * (1.0 / obs_total)

    talk(ny, gy, lambda t: y_copy(Y_CELLS, cells_send.at[t], cells_recv, t, gy).wait_send(), other)
    talk(ny, gy, lambda t: y_copy(Y_BASE, base_send.at[t], base_recv, t, gy).wait_send(), other)
    talk(ny, gy, lambda t: y_copy(Y_DEP, dsl_send.at[t], dsl_recv, t, gy).wait_send(), other)
    talk(ny, gy, lambda t: y_copy(Y_BIAS, b1_send, b1_recv, t, gy).wait_send(), other)
    talk(nx, gx, lambda t: x_copy(X_BIAS, b2_send, b2_recv, t, gx).wait_send(), other)

    def forward_x(t):
        x_copy(X_CORNER, c_send, c_recv, t, gx).wait_send()
        x_copy(X_ENDS, x_send, x_recv, t, gx).wait_send()

    def forward_y(t):
        y_copy(Y_ENDS, y_send, y_recv, t, gy).wait_send()
        y_copy(Y_CORNER, c2_send, c2_recv, t, gy).wait_send()

    def backward_x(t):
        x_copy(X_BACK_CORNER, bc_send, bc_recv, t, gx).wait_send()
        x_copy(X_CARRY, bx_send, bx_recv, t, gx).wait_send()

    def backward_y(t):
        y_copy(Y_CARRY, by_send, by_recv, t, gy).wait_send()
        y_copy(Y_BACK_CORNER, bc2_send, bc2_recv, t, gy).wait_send()

    talk(nx, gx, forward_x, later)
    talk(ny, gy, forward_y, later)
    talk(nx, gx, backward_x, earlier)
    talk(ny, gy, backward_y, earlier)


def shards(nx, ny, control, level_rate, x_rate, y_rate, jacobian, innovation, predictors, bias_coef, inv_var,
           obs_tile, obs_cell):
    variables, rows, cols, levels = control.shape
    obs, channels = innovation.shape
    by_channel = jnp.swapaxes(jacobian, 1, 2)
    cells, width = rows * cols, variables * levels
    cap = obs // 4
    kinds = predictors.shape[1]
    wide = (channels // 128 + 1) * 128
    ends = rows + cols + 8
    vmem = pl.BlockSpec(memory_space=pltpu.VMEM)
    anyw = pl.BlockSpec(memory_space=pl.ANY)
    both = lambda count, *shape: [pltpu.VMEM(shape, F32), pltpu.VMEM((count,) + shape, F32)]
    slotted = lambda *shape: [pltpu.VMEM((ny, cap) + shape, F32)] * 2
    grad, dep, bias, cost = pl.pallas_call(
        functools.partial(kernel, nx, ny),
        out_shape=(
            jax.ShapeDtypeStruct(control.shape, F32),
            jax.ShapeDtypeStruct((channels, obs), F32),
            jax.ShapeDtypeStruct((kinds, channels), F32),
            jax.ShapeDtypeStruct((1, 1), F32),
        ),
        in_specs=[anyw, vmem, vmem, vmem, anyw, anyw, vmem, vmem, vmem, vmem, vmem],
        out_specs=(vmem, vmem, vmem, vmem),
        scratch_shapes=[
            pltpu.VMEM(control.shape, F32),
            pltpu.VMEM(by_channel.shape, F32),
            pltpu.VMEM((channels, obs), F32),
            pltpu.VMEM((cells, width), BF16),
            pltpu.VMEM((cells, width), BF16),
            pltpu.VMEM((channels, width), BF16),
            pltpu.VMEM((channels, width), BF16),
            pltpu.VMEM((2, nx, 128), F32),
            pltpu.VMEM((2, ny, 128), F32),
            pltpu.VMEM((ends, width), F32),
            *both(nx, rows, width), *both(ny, cols, width), *both(nx, 1, width), *both(ny, 1, width),
            *slotted(128), *slotted(wide), *slotted(channels),
            *both(nx, rows, width), *both(ny, cols, width), *both(nx, 1, width), *both(ny, 1, width),
            pltpu.VMEM((ny, kinds, wide), F32), pltpu.VMEM((nx, kinds, wide), F32),
            pltpu.VMEM((kinds, wide), F32), pltpu.VMEM((kinds, wide), F32),
            pltpu.SemaphoreType.DMA((3,)),
            pltpu.SemaphoreType.DMA((5, nx)), pltpu.SemaphoreType.DMA((5, nx)),
            pltpu.SemaphoreType.DMA((8, ny)), pltpu.SemaphoreType.DMA((8, ny)),
        ],
        compiler_params=pltpu.CompilerParams(
            collective_id=0, has_side_effects=True, vmem_limit_bytes=60 * 1024 * 1024),
    )(control, level_rate, x_rate.reshape(1, -1), y_rate.reshape(1, -1), by_channel, innovation.T, predictors.T,
      bias_coef, inv_var, obs_tile.reshape(1, -1), obs_cell.reshape(1, -1))
    return grad, dep.T, bias, cost[0, 0]


def solution(mesh):
    nx, ny = mesh.shape["gx"], mesh.shape["gy"]
    return jax.shard_map(
        functools.partial(shards, nx, ny),
        mesh=mesh,
        in_specs=(
            P(None, "gy", "gx", None),
            P(),
            P(),
            P(),
            P(),
            P(("gx", "gy"), None),
            P(("gx", "gy"), None),
            P(),
            P(),
            P(("gx", "gy"), None),
            P(("gx", "gy")),
        ),
        out_specs=(P(None, "gy", "gx", None), P(("gx", "gy"), None), P(), P()),
        check_vma=False,
    )
```

```python
import functools

import jax
import jax.numpy as jnp
from jax import lax
from jax.experimental import pallas as pl
from jax.experimental.pallas import tpu as pltpu
from jax.sharding import PartitionSpec as P

MESH = pl.DeviceIdType.MESH
F32 = jnp.float32
BF16 = jnp.bfloat16
CUT = -1e30

X_ENDS, X_CORNER, X_CARRY, X_BACK_CORNER, X_BIAS = range(5)
Y_CELLS, Y_ENDS, Y_CORNER, Y_BASE, Y_PROF, Y_BIAS, Y_CARRY, Y_BACK_CORNER = range(8)


def iota(shape, axis):
    return lax.broadcasted_iota(jnp.int32, shape, axis)


def split(value):
    high = value.astype(BF16)
    return high, (value - high.astype(F32)).astype(BF16)


def mm(left, right, dims):
    return lax.dot_general(left, right, (dims, ((), ())), preferred_element_type=F32)


def mm3(left, right, dims=((1,), (0,))):
    (lh, ll), (rh, rl) = left, right
    return mm(lh, rh, dims) + (mm(lh, rl, dims) + mm(ll, rh, dims))


def to_col(row):
    size = row.shape[1]
    diag = iota((size, size), 0) == iota((size, size), 1)
    return jnp.sum(jnp.where(diag, row, 0.0), axis=1, keepdims=True)


def logs(rates):
    decays = 1.0 - rates
    return jnp.log(decays), 0.5 * jnp.log(1.0 - decays * decays)


def sums_both(row, start):
    size = row.shape[1]
    at0, at1 = iota((size, size), 0), iota((size, size), 1)
    as_row = jnp.sum(jnp.where((at0 <= at1) & (at0 >= start), to_col(row), 0.0), axis=0, keepdims=True)
    as_col = jnp.sum(jnp.where((at1 <= at0) & (at1 >= start), row, 0.0), axis=1, keepdims=True)
    return as_row, as_col


def between(row, me, count, width):
    size = row.shape[1]
    other, lane = iota((count, size), 0), iota((count, size), 1)
    after = (lane >= (other + 1) * width) & (lane < me * width)
    before = (lane >= (me + 1) * width) & (lane < other * width)
    fwd = jnp.exp(jnp.sum(jnp.where(after, row, 0.0), axis=1, keepdims=True))
    bwd = jnp.exp(jnp.sum(jnp.where(before, row, 0.0), axis=1, keepdims=True))
    return fwd, bwd


def kernel(
    nx, ny, control, level_rate, x_rate, y_rate, jacobian, innovation, pred_t, bias_coef, inv_var, tile_row,
    cell_row, grad_out, dep_out, bias_out, cost_out,
    state, jac, innov, state_h, state_l, jf_h, jf_l, decay_x, decay_y, carry,
    x_send, x_recv, y_send, y_recv, c_send, c_recv, c2_send, c2_recv,
    cells_send, cells_recv, base_send, base_recv, prof_send, prof_recv,
    bx_send, bx_recv, by_send, by_recv, bc_send, bc_recv, bc2_send, bc2_recv,
    b1_recv, b2_recv, b1_send, b2_send, local_sem, sx_sem, rx_sem, sy_sem, ry_sem,
):
    gx, gy = lax.axis_index("gx"), lax.axis_index("gy")
    variables, rows, cols, levels = control.shape
    cells = rows * cols
    channels, obs = innovation.shape
    cap = base_send.shape[1]
    kinds = pred_t.shape[0]
    slots = ny * cap
    width = variables * levels
    ends = rows + cols + 8

    loads = [
        pltpu.make_async_copy(control, state, local_sem.at[0]),
        pltpu.make_async_copy(jacobian, jac, local_sem.at[1]),
        pltpu.make_async_copy(innovation, innov, local_sem.at[2]),
    ]
    for at in (2, 0, 1):
        loads[at].start()

    barrier = pltpu.get_barrier_semaphore()

    def each(count, me, act, when):
        def body(t, _):
            @pl.when(when(t, me))
            def _():
                act(t)
            return 0
        lax.fori_loop(0, count, body, 0)

    other = lambda t, me: t != me
    later = lambda t, me: t > me
    earlier = lambda t, me: t < me

    def greet_x(t):
        pl.semaphore_signal(barrier, inc=1, device_id=(t, gy), device_id_type=MESH)

    def greet_y(t):
        pl.semaphore_signal(barrier, inc=1, device_id=(gx, t), device_id_type=MESH)

    each(nx, gx, greet_x, other)
    each(ny, gy, greet_y, other)

    def x_copy(row, src, dst, target, slot):
        return pltpu.make_async_remote_copy(
            src_ref=src, dst_ref=dst.at[slot], send_sem=sx_sem.at[row, target], recv_sem=rx_sem.at[row, slot],
            device_id=(target, gy), device_id_type=MESH)

    def y_copy(row, src, dst, target, slot):
        return pltpu.make_async_remote_copy(
            src_ref=src, dst_ref=dst.at[slot], send_sem=sy_sem.at[row, target], recv_sem=ry_sem.at[row, slot],
            device_id=(gx, target), device_id_type=MESH)

    tile_r = tile_row[...].astype(F32)
    cell_r = cell_row[...].astype(F32)
    tile_c = to_col(tile_r)
    at0, at1 = iota((obs, obs), 0), iota((obs, obs), 1)
    same = tile_c == tile_r
    rank_r = jnp.sum(jnp.where(same & (at0 < at1), 1.0, 0.0), axis=0, keepdims=True)
    slot_r = (tile_r * cap + rank_r).astype(jnp.int32)
    placed_t = slot_r == iota((slots, obs), 0)
    placing_t = jnp.where(placed_t, 1.0, 0.0).astype(BF16)
    sent = jnp.sum(jnp.where(placed_t, cell_r + 1.0, 0.0), axis=1, keepdims=True)
    cells_send[...] = jnp.broadcast_to(sent, (slots, 128)).reshape(ny, cap, 128)
    cells_recv[gy] = cells_send[gy]

    nn, nt, tn = ((1,), (0,)), ((1,), (1,)), ((0,), (0,))
    loads[2].wait()
    pred = split(pred_t[...])
    base = innov[...] - mm3(split(bias_coef[...]), pred, tn)
    base_parts = split(base)
    to_slots = lambda parts: mm(placing_t, parts[0], nt) + mm(placing_t, parts[1], nt)
    base_send[:, :, 0:channels] = to_slots(base_parts).reshape(ny, cap, channels)
    base_send[:, :, channels:channels + kinds] = to_slots(pred).reshape(ny, cap, kinds)
    rest = base_send.shape[2] - channels - kinds
    base_send[:, :, channels + kinds:] = jnp.zeros((ny, cap, rest), F32)
    pl.semaphore_wait(barrier, nx + ny - 2)
    talk = each
    talk(ny, gy, lambda t: y_copy(Y_CELLS, cells_send.at[t], cells_recv, t, gy).start(), other)
    talk(ny, gy, lambda t: y_copy(Y_BASE, base_send.at[t], base_recv, t, gy).start(), other)
    base_recv[gy] = base_send[gy]
    innov[...] = base

    x_log, x_scale = logs(x_rate[...])
    y_log, y_scale = logs(y_rate[...])
    fwd, bwd = between(x_log, gx, nx, cols)
    decay_x[0] = jnp.broadcast_to(fwd, (nx, 128))
    decay_x[1] = jnp.broadcast_to(bwd, (nx, 128))
    fwd, bwd = between(y_log, gy, ny, rows)
    decay_y[0] = jnp.broadcast_to(fwd, (ny, 128))
    decay_y[1] = jnp.broadcast_to(bwd, (ny, 128))
    sx_r, sx_c = sums_both(x_log, gx * cols)
    sy_r, sy_c = sums_both(y_log, gy * rows)
    qx_c = sx_c - to_col(x_scale)
    qy_c = sy_c - to_col(y_scale)

    def total(row, start, size):
        lane = iota(row.shape, 1)
        return jnp.sum(jnp.where((lane >= start) & (lane < start + size), row, 0.0), axis=1, keepdims=True)

    t_x, t_y = total(x_log, gx * cols, cols), total(y_log, gy * rows, rows)

    n = iota((1, cells), 1)
    y_n = n // cols
    x_n = n - y_n * cols

    def pick_rows(col, at):
        return jnp.sum(jnp.where(iota((col.shape[0], at.shape[1]), 0) == at, col, 0.0), axis=0, keepdims=True)

    qx_n = pick_rows(qx_c, x_n + gx * cols)
    qy_n = pick_rows(qy_c, y_n + gy * rows)
    e = iota((ends, 1), 0)
    on_x = (e < rows) & (e == y_n)
    on_y = (e >= rows) & (e - rows == x_n) & (e < rows + cols)
    to_x, to_y = t_x - qx_n, t_y - qy_n
    e_log = jnp.where(on_x, to_x, jnp.where(on_y, to_y, jnp.where(e == rows + cols, to_x + to_y, CUT)))
    e_parts = split(jnp.exp(e_log))

    loads[0].wait()
    for v in range(variables):
        high, low = split(state[v].reshape(cells, levels))
        state_h[:, v * levels:(v + 1) * levels] = high
        state_l[:, v * levels:(v + 1) * levels] = low
    field = (state_h[...], state_l[...])
    tails = mm3(e_parts, field)
    x_send[...] = tails[0:rows]
    y_send[...] = tails[rows:rows + cols]
    c_send[...] = tails[rows + cols:rows + cols + 1]
    talk(nx, gx, lambda t: x_copy(X_CORNER, c_send, c_recv, t, gx).start(), later)
    talk(nx, gx, lambda t: x_copy(X_ENDS, x_send, x_recv, t, gx).start(), later)
    talk(ny, gy, lambda t: y_copy(Y_ENDS, y_send, y_recv, t, gy).start(), later)

    carry[...] = jnp.zeros_like(carry)

    def widen(ref, side, t):
        row = ref[side, pl.ds(t, 1), :]
        return jnp.concatenate([row] * (width // 128), axis=1)

    talk(ny, gy, lambda t: y_copy(Y_CELLS, cells_send.at[t], cells_recv, t, t).wait_recv(), other)
    landed = cells_recv[...].reshape(slots, 128)[:, 0:1] - 1.0
    y_s = jnp.floor((landed + 0.5) * (1.0 / cols))
    x_s = (landed - y_s * cols).astype(jnp.int32)
    y_s = jnp.where(landed < 0.0, -5.0, y_s).astype(jnp.int32)

    def pick_cols(row, at):
        return jnp.sum(jnp.where(iota((at.shape[0], row.shape[1]), 1) == at, row, 0.0), axis=1, keepdims=True)

    sx_s = pick_cols(sx_r, x_s + gx * cols)
    sy_s = pick_cols(sy_r, jnp.where(y_s < 0, -1, y_s + gy * rows))
    reach = (y_n <= y_s) & (x_n <= x_s)
    w_cells = split(jnp.exp(jnp.where(reach, (sy_s + sx_s) - (qy_n + qx_n), CUT)))
    c = iota((1, ends), 1)
    qy_e = pick_rows(qy_c, jnp.where(c < rows, c + gy * rows, -1))
    qx_e = pick_rows(qx_c, jnp.where((c >= rows) & (c < rows + cols), c - rows + gx * cols, -1))
    y_e = jnp.where(c < rows, c, -1)
    x_e = jnp.where((c >= rows) & (c < rows + cols), c - rows, -1)
    reach_e = (y_e <= y_s) & (x_e <= x_s) & (y_s >= 0) & (c <= rows + cols)
    w_carry = split(jnp.exp(jnp.where(reach_e, (sy_s + sx_s) - (qy_e + qx_e), CUT)))

    def add_corner(t):
        x_copy(X_CORNER, c_send, c_recv, t, t).wait_recv()
        carry[rows + cols:rows + cols + 1, :] += widen(decay_x, 0, t) * c_recv[t]

    talk(nx, gx, add_corner, earlier)
    c2_send[...] = carry[rows + cols:rows + cols + 1, :]
    talk(ny, gy, lambda t: y_copy(Y_CORNER, c2_send, c2_recv, t, gy).start(), later)
    carry[rows + cols:rows + cols + 1, :] = jnp.zeros((1, width), F32)

    prof = mm3(w_cells, field)

    loads[1].wait()
    l_log, l_scale = logs(level_rate[...])
    m0, m1 = iota((levels, levels), 0), iota((levels, levels), 1)
    for v in range(variables):
        s_r, s_c = sums_both(l_log[v:v + 1, :], 0)
        q_r = s_r - l_scale[v:v + 1, :]
        f_v = split(jnp.exp(jnp.where(m1 <= m0, s_c - q_r, CUT)))
        high, low = split(mm3(split(jac[v]), f_v))
        jf_h[:, v * levels:(v + 1) * levels] = high
        jf_l[:, v * levels:(v + 1) * levels] = low

    def add_x(t):
        x_copy(X_ENDS, x_send, x_recv, t, t).wait_recv()
        carry[0:rows, :] += widen(decay_x, 0, t) * x_recv[t]

    def add_y(t):
        y_copy(Y_ENDS, y_send, y_recv, t, t).wait_recv()
        carry[rows:rows + cols, :] += widen(decay_y, 0, t) * y_recv[t]

    def add_c2(t):
        y_copy(Y_CORNER, c2_send, c2_recv, t, t).wait_recv()
        carry[rows + cols:rows + cols + 1, :] += widen(decay_y, 0, t) * c2_recv[t]

    talk(ny, gy, add_y, earlier)
    talk(nx, gx, add_x, earlier)
    talk(ny, gy, add_c2, earlier)
    prof = prof + mm3(w_carry, split(carry[...]))
    prof_send[...] = prof.reshape(ny, cap, width)
    talk(ny, gy, lambda t: y_copy(Y_PROF, prof_send.at[t], prof_recv, t, gy).start(), other)
    prof_recv[gy] = prof_send[gy]

    talk(ny, gy, lambda t: y_copy(Y_BASE, base_send.at[t], base_recv, t, t).wait_recv(), other)
    arrived = base_recv[...]
    jf = (jf_h[...], jf_l[...])
    departures = arrived[:, :, 0:channels].reshape(slots, channels) - mm3(split(prof), jf, nt)
    weighted = departures * inv_var[...].reshape(1, channels)
    w_parts = split(weighted)
    grads = split(mm3(w_parts, jf))
    out = mm3(w_carry, grads, tn)
    bx_send[...] = out[0:rows]
    by_send[...] = out[rows:rows + cols]
    bc_send[...] = out[rows + cols:rows + cols + 1]
    talk(nx, gx, lambda t: x_copy(X_BACK_CORNER, bc_send, bc_recv, t, gx).start(), earlier)
    talk(nx, gx, lambda t: x_copy(X_CARRY, bx_send, bx_recv, t, gx).start(), earlier)
    talk(ny, gy, lambda t: y_copy(Y_CARRY, by_send, by_recv, t, gy).start(), earlier)

    b1_send[:, 0:channels] = -mm3(split(arrived[:, :, channels:channels + kinds].reshape(slots, kinds)), w_parts, tn)
    cost = jnp.sum(jnp.sum(departures * weighted, axis=1, keepdims=True), axis=0, keepdims=True)
    b1_send[:, channels:] = jnp.broadcast_to(0.5 * cost, (b1_send.shape[0], b1_send.shape[1] - channels))
    talk(ny, gy, lambda t: y_copy(Y_BIAS, b1_send, b1_recv, t, gy).start(), other)
    b1_recv[gy] = b1_send[...]

    talk(ny, gy, lambda t: y_copy(Y_BIAS, b1_send, b1_recv, t, t).wait_recv(), other)
    b2_send[...] = jnp.sum(b1_recv[...], axis=0)
    talk(nx, gx, lambda t: x_copy(X_BIAS, b2_send, b2_recv, t, gx).start(), other)
    b2_recv[gx] = b2_send[...]

    carry[...] = jnp.zeros_like(carry)

    def back_corner(t):
        x_copy(X_BACK_CORNER, bc_send, bc_recv, t, t).wait_recv()
        carry[rows + cols:rows + cols + 1, :] += widen(decay_x, 1, t) * bc_recv[t]

    talk(nx, gx, back_corner, later)
    bc2_send[...] = carry[rows + cols:rows + cols + 1, :]
    talk(ny, gy, lambda t: y_copy(Y_BACK_CORNER, bc2_send, bc2_recv, t, gy).start(), earlier)
    carry[rows + cols:rows + cols + 1, :] = jnp.zeros((1, width), F32)

    here = mm3(w_cells, grads, tn)

    talk(ny, gy, lambda t: y_copy(Y_PROF, prof_send.at[t], prof_recv, t, t).wait_recv(), other)
    back_parts = split(prof_recv[...].reshape(slots, width))
    own = tuple(mm(placing_t, part, tn).astype(BF16) for part in back_parts)
    dep_out[...] = innov[...] - mm3(jf, own, nt)

    def back_x(t):
        x_copy(X_CARRY, bx_send, bx_recv, t, t).wait_recv()
        carry[0:rows, :] += widen(decay_x, 1, t) * bx_recv[t]

    def back_y(t):
        y_copy(Y_CARRY, by_send, by_recv, t, t).wait_recv()
        carry[rows:rows + cols, :] += widen(decay_y, 1, t) * by_recv[t]

    def back_c2(t):
        y_copy(Y_BACK_CORNER, bc2_send, bc2_recv, t, t).wait_recv()
        carry[rows + cols:rows + cols + 1, :] += widen(decay_y, 1, t) * bc2_recv[t]

    talk(ny, gy, back_y, later)
    talk(nx, gx, back_x, later)
    talk(ny, gy, back_c2, later)
    here = here + mm3(e_parts, split(carry[...]), tn)
    for v in range(variables):
        grad_out[v] = here[:, v * levels:(v + 1) * levels].reshape(rows, cols, levels)

    talk(nx, gx, lambda t: x_copy(X_BIAS, b2_send, b2_recv, t, t).wait_recv(), other)
    summed = jnp.sum(b2_recv[...], axis=0)
    obs_total = obs * nx * ny
    bias_out[...] = summed[:, 0:channels] * obs_total ** -0.5
    cost_out[...] = summed[0:1, channels:channels + 1] * (1.0 / obs_total)

    talk(ny, gy, lambda t: y_copy(Y_CELLS, cells_send.at[t], cells_recv, t, gy).wait_send(), other)
    talk(ny, gy, lambda t: y_copy(Y_BASE, base_send.at[t], base_recv, t, gy).wait_send(), other)
    talk(ny, gy, lambda t: y_copy(Y_PROF, prof_send.at[t], prof_recv, t, gy).wait_send(), other)
    talk(ny, gy, lambda t: y_copy(Y_BIAS, b1_send, b1_recv, t, gy).wait_send(), other)
    talk(nx, gx, lambda t: x_copy(X_BIAS, b2_send, b2_recv, t, gx).wait_send(), other)

    def forward_x(t):
        x_copy(X_CORNER, c_send, c_recv, t, gx).wait_send()
        x_copy(X_ENDS, x_send, x_recv, t, gx).wait_send()

    def forward_y(t):
        y_copy(Y_ENDS, y_send, y_recv, t, gy).wait_send()
        y_copy(Y_CORNER, c2_send, c2_recv, t, gy).wait_send()

    def backward_x(t):
        x_copy(X_BACK_CORNER, bc_send, bc_recv, t, gx).wait_send()
        x_copy(X_CARRY, bx_send, bx_recv, t, gx).wait_send()

    def backward_y(t):
        y_copy(Y_CARRY, by_send, by_recv, t, gy).wait_send()
        y_copy(Y_BACK_CORNER, bc2_send, bc2_recv, t, gy).wait_send()

    talk(nx, gx, forward_x, later)
    talk(ny, gy, forward_y, later)
    talk(nx, gx, backward_x, earlier)
    talk(ny, gy, backward_y, earlier)


def shards(nx, ny, control, level_rate, x_rate, y_rate, jacobian, innovation, predictors, bias_coef, inv_var,
           obs_tile, obs_cell):
    variables, rows, cols, levels = control.shape
    obs, channels = innovation.shape
    by_channel = jnp.swapaxes(jacobian, 1, 2)
    cells, width = rows * cols, variables * levels
    cap = obs // 4
    kinds = predictors.shape[1]
    wide = (channels // 128 + 1) * 128
    ends = rows + cols + 8
    vmem = pl.BlockSpec(memory_space=pltpu.VMEM)
    anyw = pl.BlockSpec(memory_space=pl.ANY)
    both = lambda count, *shape: [pltpu.VMEM(shape, F32), pltpu.VMEM((count,) + shape, F32)]
    slotted = lambda *shape: [pltpu.VMEM((ny, cap) + shape, F32)] * 2
    grad, dep, bias, cost = pl.pallas_call(
        functools.partial(kernel, nx, ny),
        out_shape=(
            jax.ShapeDtypeStruct(control.shape, F32),
            jax.ShapeDtypeStruct((channels, obs), F32),
            jax.ShapeDtypeStruct((kinds, channels), F32),
            jax.ShapeDtypeStruct((1, 1), F32),
        ),
        in_specs=[anyw, vmem, vmem, vmem, anyw, anyw, vmem, vmem, vmem, vmem, vmem],
        out_specs=(vmem, vmem, vmem, vmem),
        scratch_shapes=[
            pltpu.VMEM(control.shape, F32),
            pltpu.VMEM(by_channel.shape, F32),
            pltpu.VMEM((channels, obs), F32),
            pltpu.VMEM((cells, width), BF16),
            pltpu.VMEM((cells, width), BF16),
            pltpu.VMEM((channels, width), BF16),
            pltpu.VMEM((channels, width), BF16),
            pltpu.VMEM((2, nx, 128), F32),
            pltpu.VMEM((2, ny, 128), F32),
            pltpu.VMEM((ends, width), F32),
            *both(nx, rows, width), *both(ny, cols, width), *both(nx, 1, width), *both(ny, 1, width),
            *slotted(128), *slotted(wide), *slotted(width),
            *both(nx, rows, width), *both(ny, cols, width), *both(nx, 1, width), *both(ny, 1, width),
            pltpu.VMEM((ny, kinds, wide), F32), pltpu.VMEM((nx, kinds, wide), F32),
            pltpu.VMEM((kinds, wide), F32), pltpu.VMEM((kinds, wide), F32),
            pltpu.SemaphoreType.DMA((3,)),
            pltpu.SemaphoreType.DMA((5, nx)), pltpu.SemaphoreType.DMA((5, nx)),
            pltpu.SemaphoreType.DMA((8, ny)), pltpu.SemaphoreType.DMA((8, ny)),
        ],
        compiler_params=pltpu.CompilerParams(
            collective_id=0, has_side_effects=True, vmem_limit_bytes=60 * 1024 * 1024),
    )(control, level_rate, x_rate.reshape(1, -1), y_rate.reshape(1, -1), by_channel, innovation.T, predictors.T,
      bias_coef, inv_var, obs_tile.reshape(1, -1), obs_cell.reshape(1, -1))
    return grad, dep.T, bias, cost[0, 0]


def solution(mesh):
    nx, ny = mesh.shape["gx"], mesh.shape["gy"]
    return jax.shard_map(
        functools.partial(shards, nx, ny),
        mesh=mesh,
        in_specs=(
            P(None, "gy", "gx", None),
            P(),
            P(),
            P(),
            P(),
            P(("gx", "gy"), None),
            P(("gx", "gy"), None),
            P(),
            P(),
            P(("gx", "gy"), None),
            P(("gx", "gy")),
        ),
        out_specs=(P(None, "gy", "gx", None), P(("gx", "gy"), None), P(), P()),
        check_vma=False,
    )
```
